512 devices in a mesh: blk: 256 (over z, x_hi, y, core), seg: 2 (over x_lo).
Axes of the slice: x: 4 (x_hi: 2, x_lo: 2; x = x_hi * 2 + x_lo), y: 8, z: 8, core: 2. Of those that a mesh axis runs over, the one named last changes fastest.
Arguments:
- traces: float32 [4096, 16, 1024], P('blk', 'seg'), may hold values from -1140 to 1140
- mask: int32 [4096, 4, 16], P('blk'), may hold values from 0 to 1, as said below
- plan: int32 [256, 4], P('blk'), may hold values from 0 to 3, each once within a row
Outputs:
- correlations: bfloat16 [4, 4096, 16, 512], P('seg', 'blk')
The draws below stay inside these ranges and needn't reach their ends.
Inputs may be any that keep to these rules, and one draw needn't show every extreme that they name: A channel is never paired with itself: mask[a 16 + i, 0, i] is 0. Each row of plan names every distance 0 to 3 once.
All inputs are finite; a program needn't handle non-finite values.
Results may differ from the reference program's by a relative error of at most 0.011.
Values may be sent and summed in bfloat16 or wider, within the bound.
No kernel may reach another device: no remote copies, remote signals or barrier semaphores. Data moves between devices by JAX's collectives and lax.ppermute only.
A program may use at most 64 MiB of HBM per device.

```python
import math
import jax
import jax.numpy as jnp
from jax import lax

CH_DEV = 16
W_DEV = 8
SLICE_LENGTH = 1024
STEPS = 4
BOXCAR_RADIUS = 64
LAGS = 512
BLOCKS = 256
SENSOR_COUNT = 4096
RECORD_SLICES = 16
N_SEG = 2


def draw_traces(key, part):
    stochastic_seeds = jax.random.split(key, 4)
    shape = (SENSOR_COUNT, RECORD_SLICES, SLICE_LENGTH)
    noise = jnp.clip(jax.random.normal(stochastic_seeds[0], shape, jnp.float32), -6.0, 6.0)
    coeff = jax.random.uniform(stochastic_seeds[1], (SENSOR_COUNT, 1, 1), jnp.float32, -0.9, 0.9)
    earlier = jnp.concatenate([jnp.zeros((SENSOR_COUNT, RECORD_SLICES, 1), jnp.float32), noise[:, :, :-1]], axis=2)
    colored = noise + coeff * earlier
    transient_spikes = jnp.exp(jax.random.uniform(stochastic_seeds[2], (SENSOR_COUNT, RECORD_SLICES, SLICE_LENGTH // BOXCAR_RADIUS), jnp.float32, 0.0, math.log(10.0)))
    moving_amplitude_level = jnp.repeat(transient_spikes, BOXCAR_RADIUS, axis=2)
    gains = jnp.exp(jax.random.uniform(stochastic_seeds[3], (SENSOR_COUNT, 1, 1), jnp.float32, 0.0, math.log(10.0)))
    return (colored * moving_amplitude_level * gains).astype(jnp.float32)


def draw_mask(key, part):
    bits = jax.random.randint(key, (SENSOR_COUNT, STEPS, CH_DEV), 0, 2, dtype=jnp.int32)
    channel = jnp.arange(SENSOR_COUNT, dtype=jnp.int32)[:, None, None] % CH_DEV
    distance = jnp.arange(STEPS, dtype=jnp.int32)[None, :, None]
    partner = jnp.arange(CH_DEV, dtype=jnp.int32)[None, None, :]
    itself = (distance == 0) & (channel == partner)
    return jnp.where(itself, 0, bits).astype(jnp.int32)


def setup_inputs(seed: int = 0) -> dict:
    key_of = jax.random.split(jax.random.key(seed), 4)
    traces = draw_traces(jax.random.fold_in(key_of[3], 71), 0)
    mask = draw_mask(jax.random.fold_in(key_of[3], 71), 0)
    plan = jax.vmap(lambda own: jax.random.permutation(own, STEPS))(jax.random.split(key_of[2], BLOCKS)).reshape((BLOCKS, STEPS)).astype(jnp.int32)
    return dict(traces=traces, mask=mask, plan=plan)


EPS = 1e-05

def angle_table(rows, cols, length):
    left = jnp.arange(rows, dtype=jnp.int32)[:, None]
    right = jnp.arange(cols, dtype=jnp.int32)[None, :]
    product = left * right % (2 * length)
    return product.astype(jnp.float32) * (math.pi / length)

def box_table(length, half):
    left = jnp.arange(length, dtype=jnp.int32)[:, None]
    right = jnp.arange(length, dtype=jnp.int32)[None, :]
    return (jnp.abs(left - right) <= half).astype(jnp.bfloat16)

def matmul(left, right):
    return jnp.dot(left.astype(jnp.float32), right.astype(jnp.float32), preferred_element_type=jnp.float32)

def spectra_of(window_rows, length, half):
    box = box_table(length, half)
    magnitude = jnp.abs(window_rows).astype(jnp.bfloat16)
    level = matmul(magnitude, box) / (2 * half + 1)
    normed = (window_rows / (level + EPS)).astype(jnp.bfloat16)
    angles = angle_table(length, length, length)
    cos_tab = jnp.cos(angles).astype(jnp.bfloat16)
    sin_tab = (-jnp.sin(angles)).astype(jnp.bfloat16)
    spec_re = matmul(normed, cos_tab)
    spec_im = matmul(normed, sin_tab)
    amplitude = jnp.sqrt(spec_re * spec_re + spec_im * spec_im).astype(jnp.bfloat16)
    smooth = matmul(amplitude, box) / (2 * half + 1)
    return ((spec_re / (smooth + EPS)).astype(jnp.bfloat16), (spec_im / (smooth + EPS)).astype(jnp.bfloat16))

def lag_table(length, lags, windows):
    angles = angle_table(length, lags, length)
    bins = jnp.arange(length, dtype=jnp.int32)[:, None]
    weight = jnp.where(bins == 0, 1.0, 2.0).astype(jnp.float32)
    return (weight * jnp.cos(angles) / math.sqrt(windows * length)).astype(jnp.bfloat16)

def reference(traces, mask, plan):
    rows = CH_DEV * RECORD_SLICES
    flat = traces.reshape(BLOCKS, rows, SLICE_LENGTH)
    white_re, white_im = lax.map(lambda block: spectra_of(block, SLICE_LENGTH, BOXCAR_RADIUS), flat)
    padding = jnp.zeros((STEPS - 1, rows, SLICE_LENGTH), jnp.bfloat16)
    white_re = jnp.concatenate([white_re, padding], axis=0).reshape(BLOCKS + STEPS - 1, CH_DEV, RECORD_SLICES, SLICE_LENGTH)
    white_im = jnp.concatenate([white_im, padding], axis=0).reshape(BLOCKS + STEPS - 1, CH_DEV, RECORD_SLICES, SLICE_LENGTH)
    lag_tab = lag_table(SLICE_LENGTH, LAGS, RECORD_SLICES)
    block_mask = mask.reshape(BLOCKS, CH_DEV, STEPS, CH_DEV)

    def one_block(block):
        own_re = lax.dynamic_index_in_dim(white_re, block, 0, keepdims=False).astype(jnp.float32)
        own_im = lax.dynamic_index_in_dim(white_im, block, 0, keepdims=False).astype(jnp.float32)
        pair_mask = lax.dynamic_index_in_dim(block_mask, block, 0, keepdims=False).astype(jnp.float32)
        stacked = []
        for distance in range(STEPS):
            far_re = lax.dynamic_index_in_dim(white_re, block + distance, 0, keepdims=False).astype(jnp.float32)
            far_im = lax.dynamic_index_in_dim(white_im, block + distance, 0, keepdims=False).astype(jnp.float32)
            total = jnp.zeros((CH_DEV, CH_DEV, LAGS), jnp.float32)
            for segment in range(N_SEG):
                low = segment * W_DEV
                high = low + W_DEV
                cross = jnp.einsum('iwk,jwk->ijk', own_re[:, low:high], far_re[:, low:high])
                cross = cross + jnp.einsum('iwk,jwk->ijk', own_im[:, low:high], far_im[:, low:high])
                cross = cross.astype(jnp.bfloat16)
                folded = matmul(cross.reshape(CH_DEV * CH_DEV, SLICE_LENGTH), lag_tab).reshape(CH_DEV, CH_DEV, LAGS)
                folded = folded * pair_mask[:, distance, :][:, :, None]
                rounded = lax.optimization_barrier(folded.astype(jnp.bfloat16))
                total = total + rounded.astype(jnp.float32)
            stacked.append(total)
        stacked = jnp.stack(stacked)
        order = lax.dynamic_index_in_dim(plan, block, 0, keepdims=False)
        return jnp.take(stacked, order, axis=0).astype(jnp.bfloat16)
    result = lax.map(one_block, jnp.arange(BLOCKS, dtype=jnp.int32))
    return jnp.transpose(result, (1, 0, 2, 3, 4)).reshape(STEPS, SENSOR_COUNT, CH_DEV, LAGS)
```

```python
import functools
import math

import jax
import jax.numpy as jnp
from jax import lax
from jax.experimental import pallas as pl
from jax.experimental.pallas import tpu as pltpu
from jax.sharding import PartitionSpec as P

EPS = 1e-05
STEPS = 4
F32 = jnp.float32
BF16 = jnp.bfloat16
VMEM = pl.BlockSpec(memory_space=pltpu.VMEM)
SMEM = pl.BlockSpec(memory_space=pltpu.SMEM)


def angle_table(rows, cols, length):
    left = jnp.arange(rows, dtype=jnp.int32)[:, None]
    right = jnp.arange(cols, dtype=jnp.int32)[None, :]
    product = left * right % (2 * length)
    return product.astype(F32) * (math.pi / length)


def lag_table(length, lags, windows):
    angles = angle_table(length, lags, length)
    bins = jnp.arange(length, dtype=jnp.int32)[:, None]
    weight = jnp.where(bins == 0, 1.0, 2.0).astype(F32)
    return (weight * jnp.cos(angles) / math.sqrt(windows * length)).astype(BF16)


def box_sum(values, col, width, half):
    length = values.shape[1]
    low = max(0, col - 128)
    high = min(length, col + width + 128)
    left = low + lax.broadcasted_iota(jnp.int32, (high - low, width), 0)
    right = col + lax.broadcasted_iota(jnp.int32, (high - low, width), 1)
    box = jnp.where(jnp.abs(left - right) <= half, 1.0, 0.0).astype(BF16)
    return jnp.dot(values[:, low:high], box, preferred_element_type=F32)


def normalize_kernel(half, traces_ref, out_ref, rows_ref, mag_ref):
    chans, wins, length = traces_ref.shape
    for w in range(wins):
        rows = traces_ref[:, w, :]
        rows_ref[w * chans : (w + 1) * chans, :] = rows
        mag_ref[w * chans : (w + 1) * chans, :] = jnp.abs(rows).astype(BF16)
    width = 256
    for col in range(0, length, width):
        level = box_sum(mag_ref, col, width, half) / (2 * half + 1)
        part = rows_ref[:, col : col + width] / (level + EPS)
        out_ref[:, col : col + width] = part.astype(BF16)


def whiten_into(x_ref, cos_ref, sin_ref, amp_ref, re_ref, im_ref, half):
    rows, length = x_ref.shape
    mid = length // 2
    width = 256
    low = x_ref[:, :mid]
    high = x_ref[:, mid:]
    lane = lax.broadcasted_iota(jnp.int32, (1, width), 1)
    even = (lane & 1) == 0
    sign = (1 - (lane & 2)).astype(F32)
    for col in range(0, length, width):
        cols = slice(col, col + width)
        cos_low = jnp.dot(low, cos_ref[:, cols], preferred_element_type=F32)
        sin_low = jnp.dot(low, sin_ref[:, cols], preferred_element_type=F32)
        cos_high = jnp.dot(high, cos_ref[:, cols], preferred_element_type=F32)
        sin_high = jnp.dot(high, sin_ref[:, cols], preferred_element_type=F32)
        re = cos_low + sign * jnp.where(even, cos_high, -sin_high)
        im = sin_low + sign * jnp.where(even, sin_high, cos_high)
        re_ref[:, cols] = re
        im_ref[:, cols] = im
        amp_ref[:, cols] = jnp.sqrt(re * re + im * im).astype(BF16)
    for col in range(0, length, width):
        cols = slice(col, col + width)
        smooth = box_sum(amp_ref, col, width, half) / (2 * half + 1)
        scale = 1.0 / (smooth + EPS)
        re_ref[:, cols] = (re_ref[:, cols] * scale).astype(BF16).astype(F32)
        im_ref[:, cols] = (im_ref[:, cols] * scale).astype(BF16).astype(F32)


def whiten_kernel(half, x_ref, cos_ref, sin_ref, out_ref, amp_ref):
    whiten_into(x_ref, cos_ref, sin_ref, amp_ref, out_ref.at[0], out_ref.at[1], half)


def pairs_kernel(
    half, per_row, plan_ref, own_ref, other_ref, y2_ref, y2o_ref, near_ref, swap_ref, y3_ref, y3o_ref,
    mask_ref, cos_ref, sin_ref, lag_ref, out_ref, x_ref, amp_ref, white_ref, cross_ref,
):
    chans = 16
    half_rows = own_ref.shape[1]
    wins = half_rows // chans
    length = own_ref.shape[2]
    blk = lax.axis_index("blk")
    seg = lax.axis_index("seg")
    chip = blk // 2
    core = blk % 2
    wrap = (chip % per_row == per_row - 1).astype(jnp.int32)
    ahead = ((chip + 1) % per_row == per_row - 1).astype(jnp.int32)
    flip_of = (
        jnp.int32(0),
        jnp.where(core == 0, 0, wrap),
        wrap,
        jnp.where(core == 0, wrap, jnp.bitwise_xor(wrap, ahead)),
    )
    for h, ref in enumerate((own_ref, other_ref)):
        for c in range(2):
            white_ref[0, h, c] = ref[c]
    for n in range(out_ref.shape[0]):
        distance = plan_ref[0, seg * out_ref.shape[0] + n]
        flip = jnp.int32(0)
        for d in (1, 2, 3):
            flip = jnp.where(distance == d, flip_of[d], flip)

        def take(when, first, second):
            @pl.when(when)
            def _():
                x_ref[0] = first[...]
                x_ref[1] = second[...]

        take((distance == 1) & (core == 0), near_ref.at[0], near_ref.at[1])
        take((distance == 1) & (core == 1), near_ref.at[0], swap_ref)
        take(distance == 2, y2_ref, y2o_ref)
        take((distance == 3) & (core == 0), near_ref.at[2], swap_ref)
        take((distance == 3) & (core == 1), y3_ref, y3o_ref)

        @pl.when(distance > 0)
        def _():
            for h in range(2):
                whiten_into(x_ref.at[h], cos_ref, sin_ref, amp_ref, white_ref.at[1, h, 0], white_ref.at[1, h, 1], half)

        slot = jnp.where(distance == 0, 0, 1)
        group = 8

        def body(step, carry):
            lanes = pl.ds(pl.multiple_of(step * 128, 128), 128)
            for first in range(0, chans, group):
                sums = [jnp.zeros((chans, 128), F32) for _ in range(group)]
                for h in range(2):
                    mine = jnp.bitwise_xor(flip, h)
                    for w in range(wins):
                        for c in range(2):
                            far = white_ref[slot, h, c, w * chans : (w + 1) * chans, lanes]
                            for i in range(group):
                                at = w * chans + first + i
                                row = white_ref[0, mine, c, at : at + 1, lanes]
                                sums[i] = sums[i] + row * far
                for i in range(group):
                    at = (first + i) * chans
                    cross_ref[at : at + chans, lanes] = sums[i].astype(BF16)
            return carry

        lax.fori_loop(0, length // 128, body, 0)
        folded = jnp.dot(cross_ref[...], lag_ref[...], preferred_element_type=F32)
        keep = mask_ref[distance]
        for col in range(0, folded.shape[1], 128):
            part = folded[:, col : col + 128] * keep
            out_ref[n, :, col : col + 128] = part.astype(BF16)


def per_device(per_row, traces, mask, plan):
    chans, wins, length = traces.shape
    half = length // 16
    lags = length // 2
    rows = chans * wins
    blocks = lax.axis_size("blk")
    segs = lax.axis_size("seg")
    steps = STEPS // segs
    core = lax.axis_index("blk") % 2

    def send(array, source):
        pairs = []
        for b in range(blocks):
            for s in range(segs):
                where = source(b, s)
                if where is not None and where[0] < blocks:
                    pairs.append((where[0] * segs + where[1], b * segs + s))
        return lax.ppermute(array, ("blk", "seg"), pairs)

    def ahead(b, s, by):
        chip = b // 2
        wraps = (chip % per_row == per_row - 1) and (b + by) // 2 > chip
        return (b + by, 1 - s if wraps else s)

    angles = angle_table(length // 2, length, length)
    cos_tab = jnp.cos(angles).astype(BF16)
    sin_tab = jnp.sin(angles).astype(BF16)
    lag_tab = lag_table(length, lags, wins * segs)

    x = pl.pallas_call(
        functools.partial(normalize_kernel, half),
        out_shape=jax.ShapeDtypeStruct((rows, length), BF16),
        in_specs=[VMEM],
        out_specs=VMEM,
        scratch_shapes=[pltpu.VMEM((rows, length), F32), pltpu.VMEM((rows, length), BF16)],
        name="normalize",
    )(traces)

    def whiten(array):
        return pl.pallas_call(
            functools.partial(whiten_kernel, half),
            out_shape=jax.ShapeDtypeStruct((2, rows, length), F32),
            in_specs=[VMEM] * 3,
            out_specs=VMEM,
            scratch_shapes=[pltpu.VMEM((rows, length), BF16)],
            name="whiten",
        )(array, cos_tab, sin_tab)

    y2 = send(x, lambda b, s: ahead(b, s, 2))
    o = send(x, lambda b, s: (b, 1 - s))
    own = whiten(x)
    y3 = send(y2, lambda b, s: ahead(b, s, 1) if b % 2 else None)
    y2o = send(jnp.where(core == 0, o, y2), lambda b, s: (b, 1 - s) if b % 2 else ahead(b, s, 2))
    near = send(jnp.stack((jnp.where(core == 0, y2, x), o, y2)), lambda b, s: (b ^ 1, s))
    other = whiten(o)
    swap = send(y2o, lambda b, s: (b ^ 1, s))
    y3o = send(y3, lambda b, s: (b, 1 - s) if b % 2 else None)

    keep = jnp.transpose(mask, (1, 0, 2)).reshape(STEPS, chans * chans, 1)
    keep = jnp.broadcast_to(keep, (STEPS, chans * chans, 128)).astype(F32)

    out = pl.pallas_call(
        functools.partial(pairs_kernel, half, per_row),
        out_shape=jax.ShapeDtypeStruct((steps, chans * chans, lags), BF16),
        in_specs=[SMEM] + [VMEM] * 12,
        out_specs=VMEM,
        scratch_shapes=[
            pltpu.VMEM((2, rows, length), BF16),
            pltpu.VMEM((rows, length), BF16),
            pltpu.VMEM((2, 2, 2, rows, length), F32),
            pltpu.VMEM((chans * chans, length), BF16),
        ],
        name="pairs",
    )(plan, own, other, y2, y2o, near, swap, y3, y3o, keep, cos_tab, sin_tab, lag_tab)
    return out.reshape(steps, chans, chans, lags)


def solution(mesh):
    return jax.shard_map(
        functools.partial(per_device, 8),
        mesh=mesh,
        in_specs=(P("blk", "seg", None), P("blk", None, None), P("blk", None)),
        out_specs=P("seg", "blk", None, None),
        check_vma=False,
    )
```

```python
import functools
import math

import jax
import jax.numpy as jnp
import ml_dtypes
import numpy as np
from jax import lax
from jax.experimental import pallas as pl
from jax.experimental.pallas import tpu as pltpu
from jax.sharding import PartitionSpec as P

EPS = 1e-05
STEPS = 4
F32 = jnp.float32
BF16 = jnp.bfloat16
VMEM = pl.BlockSpec(memory_space=pltpu.VMEM)
SMEM = pl.BlockSpec(memory_space=pltpu.SMEM)
HBM = pl.BlockSpec(memory_space=pltpu.HBM)
WIDTH = 256
REACH = 128


def angle_table(rows, cols, length):
    product = np.arange(rows)[:, None] * np.arange(cols)[None, :] % (2 * length)
    return product.astype(np.float32) * np.float32(math.pi / length)


def wave_table(length):
    angles = angle_table(length // 2, length, length)
    return np.stack((np.cos(angles), np.sin(angles))).astype(ml_dtypes.bfloat16)


def fill_box(box_ref, half):
    left = lax.broadcasted_iota(jnp.int32, box_ref.shape, 0) - REACH
    right = lax.broadcasted_iota(jnp.int32, box_ref.shape, 1)
    box_ref[...] = jnp.where(jnp.abs(left - right) <= half, 1.0, 0.0).astype(BF16)


def box_sum(values, box, col):
    low = max(0, col - REACH)
    high = min(values.shape[1], col + WIDTH + REACH)
    tile = box[low - col + REACH : high - col + REACH, :]
    return jnp.dot(values[:, low:high], tile, preferred_element_type=F32)


def normalize_kernel(half, traces_hbm, out_ref, traces_ref, mag_ref, box_ref, sems):
    copies = []
    for q, col in enumerate(range(0, traces_ref.shape[1], WIDTH)):
        cols = slice(col, col + WIDTH)
        copies.append(pltpu.make_async_copy(traces_hbm.at[:, cols], traces_ref.at[:, cols], sems.at[q]))
        copies[-1].start()
    fill_box(box_ref, half)
    for q in range(len(copies) + 1):
        if q < len(copies):
            copies[q].wait()
            cols = slice(q * WIDTH, (q + 1) * WIDTH)
            mag_ref[:, cols] = jnp.abs(traces_ref[:, cols]).astype(BF16)
        if q > 0:
            cols = slice((q - 1) * WIDTH, q * WIDTH)
            level = box_sum(mag_ref, box_ref, (q - 1) * WIDTH) / (2 * half + 1)
            out_ref[:, cols] = (traces_ref[:, cols] / (level + EPS)).astype(BF16)


def start_tables(wave_hbm, wave_ref, sems):
    copies = []
    for q, col in enumerate(range(0, wave_ref.shape[2], WIDTH)):
        cols = slice(col, col + WIDTH)
        copies.append(pltpu.make_async_copy(wave_hbm.at[:, :, cols], wave_ref.at[:, :, cols], sems.at[q]))
        copies[-1].start()
    return copies


def whiten_into(x_ref, wave_ref, box_ref, amp_ref, work_ref, tile_ref, out_ref, half, copies=()):
    rows, length = x_ref.shape
    mid = length // 2
    runs = length // 128
    both = jnp.concatenate([x_ref[:, :mid], x_ref[:, mid:]], axis=0)
    lane = lax.broadcasted_iota(jnp.int32, (1, WIDTH), 1)
    even = (lane & 1) == 0
    sign = (1 - (lane & 2)).astype(F32)
    for q, col in enumerate(range(0, length, WIDTH)):
        cols = slice(col, col + WIDTH)
        if copies:
            copies[q].wait()
        cos_part = jnp.dot(both, wave_ref[0, :, cols], preferred_element_type=F32)
        sin_part = jnp.dot(both, wave_ref[1, :, cols], preferred_element_type=F32)
        re = cos_part[:rows] + sign * jnp.where(even, cos_part[rows:], -sin_part[rows:])
        im = sin_part[:rows] + sign * jnp.where(even, sin_part[rows:], cos_part[rows:])
        work_ref[0, :, cols] = re
        work_ref[1, :, cols] = im
        amp_ref[:, cols] = jnp.sqrt(re * re + im * im).astype(BF16)
    for col in range(0, length, WIDTH):
        smooth = box_sum(amp_ref, box_ref, col) / (2 * half + 1)
        scale = 1.0 / (smooth + EPS)
        for c in range(2):
            for lane in range(0, WIDTH, 128):
                run = (col + lane) // 128
                white = work_ref[c, :, col + lane : col + lane + 128] * scale[:, lane : lane + 128]
                tile_ref[pl.ds(c * runs + run, rows, stride=2 * runs), :] = white
    out_ref[...] = tile_ref[...].astype(BF16).reshape(out_ref.shape)


def whiten_kernel(half, x_ref, wave_hbm, out_ref, wave_ref, box_ref, amp_ref, work_ref, tile_ref, sems):
    copies = start_tables(wave_hbm, wave_ref, sems)
    fill_box(box_ref, half)
    whiten_into(x_ref, wave_ref, box_ref, amp_ref, work_ref, tile_ref, out_ref, half, copies)


def cross_into(mine_ref, far_ref, pair_ref, cross_ref):
    chans, wins, height, _ = mine_ref.shape
    runs = height // 2
    group = 8
    parts = chans // group

    def step(at, carry):
        i = at // parts
        part = at % parts
        mine = [mine_ref[i, w] for w in range(wins)]
        for j in range(group):
            terms = [mine[w] * far_ref[part * group + j, w] for w in range(wins)]
            while len(terms) > wins // 4:
                terms = [terms[k] + terms[k + 1] for k in range(0, len(terms), 2)]
            wide = [term.astype(F32) for term in terms]
            total = sum(wide[1:], wide[0])
            pair_ref[at, pl.ds(j, runs, stride=group), :] = total[:runs] + total[runs:]
        return carry

    lax.fori_loop(0, chans * parts, step, 0, unroll=2)
    for run in range(runs):
        tile = pair_ref[:, run * group : (run + 1) * group, :].reshape(chans * chans, 128)
        cross_ref[:, run * 128 : (run + 1) * 128] = tile.astype(BF16)


def flip_of(distance, per_row):
    blk = lax.axis_index("blk")
    chip = blk // 2
    core = blk % 2
    wrap = (chip % per_row == per_row - 1).astype(jnp.int32)
    ahead = ((chip + 1) % per_row == per_row - 1).astype(jnp.int32)
    one = jnp.where(core == 0, 0, wrap)
    three = jnp.where(core == 0, wrap, jnp.bitwise_xor(wrap, ahead))
    return jnp.where(distance == 1, one, jnp.where(distance == 2, wrap, jnp.where(distance == 3, three, 0)))


def half_kernel(half, per_row, second, scale, plan_ref, own_ref, other_ref, y13_ref, y2_ref, wave_hbm, *refs):
    if second:
        part_ref, mask_ref, out_ref = refs[:3]
        refs = refs[3:]
    else:
        out_ref = refs[0]
        refs = refs[1:]
    wave_ref, box_ref, amp_ref, x_ref, work_ref, tile_ref, mine_ref, far_ref, pair_ref, cross_ref, sems = refs
    copies = start_tables(wave_hbm, wave_ref, sems)
    fill_box(box_ref, half)
    seg = lax.axis_index("seg")

    for n in range(out_ref.shape[0]):
        distance = plan_ref[0, seg * out_ref.shape[0] + n]
        which = jnp.bitwise_xor(flip_of(distance, per_row), second)

        def copy(when, source, target):
            @pl.when(when)
            def _():
                target[...] = source[...]

        for h, ref in enumerate((own_ref, other_ref)):
            copy(which == h, ref, mine_ref)
            copy((which == h) & (distance == 0), ref, far_ref)
        for d, y_ref in ((1, y13_ref.at[0]), (2, y2_ref), (3, y13_ref.at[1])):
            copy(distance == d, y_ref, x_ref)
        if n == 0:
            for table in copies:
                table.wait()

        @pl.when(distance > 0)
        def _():
            whiten_into(x_ref, wave_ref, box_ref, amp_ref, work_ref, tile_ref, far_ref, half)

        cross_into(mine_ref, far_ref, pair_ref, cross_ref)
        folded = lax.dot_general(
            cross_ref[...], wave_ref[0], (((1,), (1,)), ((), ())), preferred_element_type=F32
        )
        once = cross_ref[:, 0:1].astype(F32)
        if second:
            keep = mask_ref[distance]
            for col in range(0, folded.shape[1], 128):
                cols = slice(col, col + 128)
                part = (2.0 * folded[:, cols] - once) * scale
                part = (part + part_ref[n, :, cols]) * keep
                out_ref[n, :, cols] = part.astype(BF16)
        else:
            out_ref[n] = (2.0 * folded - once) * scale


def per_device(per_row, traces, mask, plan):
    chans, wins, length = traces.shape
    half = length // 16
    lags = length // 2
    rows = chans * wins
    blocks = lax.axis_size("blk")
    segs = lax.axis_size("seg")
    steps = STEPS // segs
    core = lax.axis_index("blk") % 2

    def send(array, source):
        pairs = []
        for b in range(blocks):
            for s in range(segs):
                where = source(b, s)
                if where is not None and where[0] < blocks:
                    pairs.append((where[0] * segs + where[1], b * segs + s))
        return lax.ppermute(array, ("blk", "seg"), pairs)

    def ahead(b, s, by):
        chip = b // 2
        wraps = (chip % per_row == per_row - 1) and (b + by) // 2 > chip
        return (b + by, 1 - s if wraps else s)

    def in_hbm(array):
        return pltpu.with_memory_space_constraint(array, pltpu.HBM)

    wave_tab = in_hbm(jnp.asarray(wave_table(length)))
    runs = length // 128
    white_shape = (chans, wins, 2 * runs, 128)
    scale = 1.0 / math.sqrt(wins * segs * length)
    quarters = length // WIDTH
    box = pltpu.VMEM((WIDTH + 2 * REACH, WIDTH), BF16)
    wave = pltpu.VMEM(wave_tab.shape, BF16)
    amp = pltpu.VMEM((rows, length), BF16)
    work = pltpu.VMEM((2, rows, length), F32)
    tile = pltpu.VMEM((rows * 2 * runs, 128), F32)
    white = pltpu.VMEM(white_shape, BF16)

    x = pl.pallas_call(
        functools.partial(normalize_kernel, half),
        out_shape=jax.ShapeDtypeStruct((rows, length), BF16),
        in_specs=[HBM],
        out_specs=VMEM,
        scratch_shapes=[
            pltpu.VMEM((rows, length), F32),
            amp,
            box,
            pltpu.SemaphoreType.DMA((quarters,)),
        ],
        compiler_params=pltpu.CompilerParams(vmem_limit_bytes=6 << 20),
        name="normalize",
    )(in_hbm(traces.reshape(rows, length)))

    def whiten(array):
        return pl.pallas_call(
            functools.partial(whiten_kernel, half),
            out_shape=jax.ShapeDtypeStruct(white_shape, BF16),
            in_specs=[VMEM, HBM],
            out_specs=VMEM,
            scratch_shapes=[wave, box, amp, work, tile, pltpu.SemaphoreType.DMA((quarters,))],
            compiler_params=pltpu.CompilerParams(vmem_limit_bytes=12 << 20),
            name="whiten",
        )(array, wave_tab)

    def half_sums(second, dtype, *args):
        return pl.pallas_call(
            functools.partial(half_kernel, half, per_row, second, scale),
            out_shape=jax.ShapeDtypeStruct((steps, chans * chans, lags), dtype),
            in_specs=[SMEM] + [VMEM] * 4 + [HBM] + [VMEM] * (2 * second),
            out_specs=VMEM,
            scratch_shapes=[
                wave,
                box,
                amp,
                amp,
                work,
                tile,
                white,
                white,
                pltpu.VMEM((chans * chans // 8, 8 * runs, 128), F32),
                pltpu.VMEM((chans * chans, length), BF16),
                pltpu.SemaphoreType.DMA((quarters,)),
            ],
            compiler_params=pltpu.CompilerParams(vmem_limit_bytes=24 << 20),
            name="second" if second else "first",
        )(plan, own, other, *args)

    keep = jnp.transpose(mask, (1, 0, 2)).reshape(STEPS, chans * chans, 1)
    keep = jnp.broadcast_to(keep, (STEPS, chans * chans, 128)).astype(F32)

    def next_block(b, s):
        return ahead(b, s, 1) if b % 2 else (b + 1, s)

    y2 = send(x, lambda b, s: ahead(b, s, 2))
    o = send(x, lambda b, s: (b, 1 - s))
    own = whiten(x)
    y2, own = lax.optimization_barrier((y2, own))
    y2o = send(y2, lambda b, s: (b, 1 - s))
    y13 = send(jnp.stack((x, y2)), next_block)
    other = whiten(o)
    y2o, other = lax.optimization_barrier((y2o, other))
    y13o = send(jnp.stack((o, y2o)), next_block)
    part = half_sums(0, F32, y13, y2, wave_tab)
    out = half_sums(1, BF16, y13o, y2o, wave_tab, part, keep)
    return out.reshape(steps, chans, chans, lags)


def solution(mesh):
    return jax.shard_map(
        functools.partial(per_device, 8),
        mesh=mesh,
        in_specs=(P("blk", "seg", None), P("blk", None, None), P("blk", None)),
        out_specs=P("seg", "blk", None, None),
        check_vma=False,
    )
```

```python
import functools
import math

import jax
import jax.numpy as jnp
import ml_dtypes
import numpy as np
from jax import lax
from jax.experimental import pallas as pl
from jax.experimental.pallas import tpu as pltpu
from jax.sharding import PartitionSpec as P


EPS = 1e-05
TINY = 1e-30
STEPS = 4
F32 = jnp.float32
BF16 = jnp.bfloat16
VMEM = pl.BlockSpec(memory_space=pltpu.VMEM)
SMEM = pl.BlockSpec(memory_space=pltpu.SMEM)
HBM = pl.BlockSpec(memory_space=pltpu.HBM)
WIDTH = 256
REACH = 128


def angle_table(rows, cols, length):
    product = np.arange(rows)[:, None] * np.arange(cols)[None, :] % (2 * length)
    return product.astype(np.float32) * np.float32(math.pi / length)


def wave_table(length):
    angles = angle_table(length // 2, length, length)
    return np.stack((np.cos(angles), np.sin(angles))).astype(ml_dtypes.bfloat16)


def fill_box(box_ref, half):
    left = lax.broadcasted_iota(jnp.int32, box_ref.shape, 0) - REACH
    right = lax.broadcasted_iota(jnp.int32, box_ref.shape, 1)
    box_ref[...] = jnp.where(jnp.abs(left - right) <= half, 1.0, 0.0).astype(BF16)


def box_sum(values, box, col):
    low = max(0, col - REACH)
    high = min(values.shape[1], col + WIDTH + REACH)
    tile = box[low - col + REACH : high - col + REACH, :]
    return jnp.dot(values[:, low:high], tile, preferred_element_type=F32)


def normalize_kernel(half, wins, traces_hbm, out_ref, traces_ref, mag_ref, box_ref, sems):
    rows, length = traces_ref.shape
    chans = rows // wins
    copies = []
    for q, col in enumerate(range(0, length, WIDTH)):
        cols = slice(col, col + WIDTH)
        copies.append(pltpu.make_async_copy(traces_hbm.at[:, cols], traces_ref.at[:, cols], sems.at[q]))
        copies[-1].start()
    fill_box(box_ref, half)
    target = lax.broadcasted_iota(jnp.int32, (rows, rows), 0)
    source = lax.broadcasted_iota(jnp.int32, (rows, rows), 1)
    order = jnp.where(target % chans * wins + target // chans == source, 1.0, 0.0).astype(BF16)
    for q in range(len(copies) + 1):
        if q < len(copies):
            copies[q].wait()
            cols = slice(q * WIDTH, (q + 1) * WIDTH)
            mag_ref[:, cols] = jnp.abs(traces_ref[:, cols]).astype(BF16)
        if q > 0:
            cols = slice((q - 1) * WIDTH, q * WIDTH)
            level = box_sum(mag_ref, box_ref, (q - 1) * WIDTH) / (2 * half + 1)
            normed = (traces_ref[:, cols] / (level + EPS)).astype(BF16)
            out_ref[:, cols] = jnp.dot(order, normed, preferred_element_type=F32).astype(BF16)


def start_tables(wave_hbm, wave_ref, sems):
    copies = []
    for q, col in enumerate(range(0, wave_ref.shape[2], WIDTH)):
        cols = slice(col, col + WIDTH)
        copies.append(pltpu.make_async_copy(wave_hbm.at[:, :, cols], wave_ref.at[:, :, cols], sems.at[q]))
        copies[-1].start()
    return copies


def whiten_into(x_refs, wave_ref, box_ref, amp_ref, work_ref, out_refs, half, copies):
    rows, length = x_refs[0].shape
    count = len(x_refs)
    mid = length // 2
    shape = out_refs[0].shape[1:3] + (WIDTH,)
    both = jnp.concatenate([ref[:, :mid] for ref in x_refs] + [ref[:, mid:] for ref in x_refs], axis=0)
    lane = lax.broadcasted_iota(jnp.int32, (1, WIDTH), 1)
    even = (lane & 1) == 0
    sign = (1 - (lane & 2)).astype(F32)
    top = count * rows
    for q, col in enumerate(range(0, length, WIDTH)):
        cols = slice(col, col + WIDTH)
        copies[q].wait()
        cos_part = jnp.dot(both, wave_ref[0, :, cols], preferred_element_type=F32)
        sin_part = jnp.dot(both, wave_ref[1, :, cols], preferred_element_type=F32)
        re = cos_part[:top] + sign * jnp.where(even, cos_part[top:], -sin_part[top:])
        im = sin_part[:top] + sign * jnp.where(even, sin_part[top:], cos_part[top:])
        work_ref[0, :, cols] = re
        work_ref[1, :, cols] = im
        power = re * re + im * im
        amp_ref[:, cols] = (power * lax.rsqrt(jnp.maximum(power, TINY))).astype(BF16)
    for col in range(0, length, WIDTH):
        cols = slice(col, col + WIDTH)
        smooth = box_sum(amp_ref, box_ref, col) / (2 * half + 1)
        scale = 1.0 / (smooth + EPS)
        for c in range(2):
            white = work_ref[c, :, cols] * scale
            for n, ref in enumerate(out_refs):
                ref[c, :, :, cols] = white[n * rows : (n + 1) * rows].astype(ref.dtype).reshape(shape)


def whiten_kernel(half, x_ref, wave_hbm, out_ref, wave_ref, box_ref, amp_ref, work_ref, sems):
    copies = start_tables(wave_hbm, wave_ref, sems)
    fill_box(box_ref, half)
    whiten_into([x_ref], wave_ref, box_ref, amp_ref, work_ref, [out_ref], half, copies)


def cross_sums(mine_ref, far_ref, cross_ref, base):
    _, wins, chans, length = mine_ref.shape
    group = 8
    groups = chans // group

    def step(at, carry):
        lanes = pl.ds(pl.multiple_of(at // groups * 128, 128), 128)
        first = pl.multiple_of(at % groups * group, group)

        def add(w, sums):
            sums = list(sums)
            for c in range(2):
                far = far_ref[c, w, :, lanes]
                mine = mine_ref.at[c, w, pl.ds(first, group), lanes]
                for i in range(group):
                    sums[i] = sums[i] + mine[i : i + 1, :] * far
            return tuple(sums)

        zeros = tuple(jnp.zeros((chans, 128), F32) for _ in range(group))
        sums = lax.fori_loop(0, wins, add, zeros, unroll=8)
        total = jnp.concatenate(sums, axis=0).astype(BF16)
        cross_ref[pl.ds(base + pl.multiple_of(first * chans, group * chans), group * chans), lanes] = total
        return carry

    lax.fori_loop(0, length // 128 * groups, step, 0)


def flip_of(distance, per_row):
    blk = lax.axis_index("blk")
    chip = blk // 2
    core = blk % 2
    wrap = (chip % per_row == per_row - 1).astype(jnp.int32)
    ahead = ((chip + 1) % per_row == per_row - 1).astype(jnp.int32)
    one = jnp.where(core == 0, 0, wrap)
    three = jnp.where(core == 0, wrap, jnp.bitwise_xor(wrap, ahead))
    return jnp.where(distance == 1, one, jnp.where(distance == 2, wrap, jnp.where(distance == 3, three, 0)))


def half_kernel(
    half, per_row, second, scale, plan_ref, own_ref, other_ref, y1_ref, y2_ref, y3_ref, wave_hbm, *refs
):
    if second:
        part_ref, mask_ref, out_ref = refs[:3]
        refs = refs[3:]
    else:
        out_ref = refs[0]
        refs = refs[1:]
    wave_ref, box_ref, amp_ref, x_ref, work_ref, mine_ref, far_ref, cross_ref, sems = refs
    copies = start_tables(wave_hbm, wave_ref, sems)
    fill_box(box_ref, half)
    seg = lax.axis_index("seg")
    chans = own_ref.shape[2]
    wins = own_ref.shape[1]
    steps = out_ref.shape[0]
    pairs = chans * chans
    distances = [plan_ref[0, seg * steps + n] for n in range(steps)]

    for n, distance in enumerate(distances):
        which = jnp.bitwise_xor(flip_of(distance, per_row), second)
        for h, ref in enumerate((own_ref, other_ref)):

            @pl.when(which == h)
            def _(ref=ref, n=n):
                for c in range(2):
                    for w in range(wins):
                        mine_ref[n, c, w] = ref[c, w].astype(F32)

        for when, y_ref in ((distance == 1, y1_ref), (distance % 2 == 0, y2_ref), (distance == 3, y3_ref)):

            @pl.when(when)
            def _(y_ref=y_ref, n=n):
                x_ref[n] = y_ref[...]

    x_refs = [x_ref.at[n] for n in range(steps)]
    far_refs = [far_ref.at[n] for n in range(steps)]
    whiten_into(x_refs, wave_ref, box_ref, amp_ref, work_ref, far_refs, half, copies)

    for n, distance in enumerate(distances):

        @pl.when(distance == 0)
        def _(n=n):
            far_ref[n] = mine_ref[n]

        cross_sums(mine_ref.at[n], far_ref.at[n], cross_ref, n * pairs)

    lane = lax.broadcasted_iota(jnp.int32, (1, 128), 1)
    cross_ref[:, :128] = cross_ref[:, :128] * jnp.where(lane == 0, 0.5, 1.0).astype(BF16)
    folded = lax.dot_general(
        cross_ref[...], wave_ref[0], (((1,), (1,)), ((), ())), preferred_element_type=F32
    )
    for n, distance in enumerate(distances):
        rows = slice(n * pairs, (n + 1) * pairs)
        if second:
            keep = mask_ref[distance]
            for col in range(0, folded.shape[1], 128):
                cols = slice(col, col + 128)
                part = folded[rows, cols] * (2.0 * scale) + part_ref[n, :, cols]
                part = part * keep
                out_ref[n, :, cols] = part.astype(BF16)
        else:
            out_ref[n] = folded[rows] * (2.0 * scale)


def per_device(per_row, traces, mask, plan):
    chans, wins, length = traces.shape
    half = length // 16
    lags = length // 2
    rows = chans * wins
    blocks = lax.axis_size("blk")
    segs = lax.axis_size("seg")
    steps = STEPS // segs

    def send(array, source):
        pairs = []
        for b in range(blocks):
            for s in range(segs):
                where = source(b, s)
                if where is not None and where[0] < blocks:
                    pairs.append((where[0] * segs + where[1], b * segs + s))
        return lax.ppermute(array, ("blk", "seg"), pairs)

    def ahead(b, s, by):
        chip = b // 2
        wraps = (chip % per_row == per_row - 1) and (b + by) // 2 > chip
        return (b + by, 1 - s if wraps else s)

    def in_hbm(array):
        return pltpu.with_memory_space_constraint(array, pltpu.HBM)

    wave_tab = in_hbm(jnp.asarray(wave_table(length)))
    white_shape = (2, wins, chans, length)
    scale = 1.0 / math.sqrt(wins * segs * length)
    quarters = length // WIDTH
    box = pltpu.VMEM((WIDTH + 2 * REACH, WIDTH), BF16)
    wave = pltpu.VMEM(wave_tab.shape, BF16)
    amp = pltpu.VMEM((rows, length), BF16)
    work = pltpu.VMEM((2, rows, length), F32)

    x = pl.pallas_call(
        functools.partial(normalize_kernel, half, wins),
        out_shape=jax.ShapeDtypeStruct((rows, length), BF16),
        in_specs=[HBM],
        out_specs=VMEM,
        scratch_shapes=[
            pltpu.VMEM((rows, length), F32),
            amp,
            box,
            pltpu.SemaphoreType.DMA((quarters,)),
        ],
        compiler_params=pltpu.CompilerParams(vmem_limit_bytes=6 << 20),
        name="normalize",
    )(in_hbm(traces.reshape(rows, length)))

    def whiten(array):
        return pl.pallas_call(
            functools.partial(whiten_kernel, half),
            out_shape=jax.ShapeDtypeStruct(white_shape, BF16),
            in_specs=[VMEM, HBM],
            out_specs=VMEM,
            scratch_shapes=[wave, box, amp, work, pltpu.SemaphoreType.DMA((quarters,))],
            compiler_params=pltpu.CompilerParams(vmem_limit_bytes=12 << 20),
            name="whiten",
        )(array, wave_tab)

    def half_sums(second, dtype, *args):
        return pl.pallas_call(
            functools.partial(half_kernel, half, per_row, second, scale),
            out_shape=jax.ShapeDtypeStruct((steps, chans * chans, lags), dtype),
            in_specs=[SMEM] + [VMEM] * 5 + [HBM] + [VMEM] * (2 * second),
            out_specs=VMEM,
            scratch_shapes=[
                wave,
                box,
                pltpu.VMEM((steps * rows, length), BF16),
                pltpu.VMEM((steps, rows, length), BF16),
                pltpu.VMEM((2, steps * rows, length), F32),
                pltpu.VMEM((steps,) + white_shape, F32),
                pltpu.VMEM((steps,) + white_shape, F32),
                pltpu.VMEM((steps * chans * chans, length), BF16),
                pltpu.SemaphoreType.DMA((quarters,)),
            ],
            compiler_params=pltpu.CompilerParams(vmem_limit_bytes=24 << 20),
            name="second" if second else "first",
        )(plan, own, other, *args)

    keep = jnp.transpose(mask, (1, 0, 2)).reshape(STEPS, chans * chans, 1)
    keep = jnp.broadcast_to(keep, (STEPS, chans * chans, 128)).astype(F32)

    def next_block(b, s):
        return ahead(b, s, 1) if b % 2 else (b + 1, s)

    y2 = send(x, lambda b, s: ahead(b, s, 2))
    o = send(x, lambda b, s: (b, 1 - s))
    y1 = send(x, next_block)
    own = whiten(x)
    y2, own = lax.optimization_barrier((y2, own))
    y2o = send(y2, lambda b, s: (b, 1 - s))
    y3 = send(y2, next_block)
    other = whiten(o)
    y2o, other = lax.optimization_barrier((y2o, other))
    y13o = send(jnp.stack((o, y2o)), next_block)
    part = half_sums(0, F32, y1, y2, y3, wave_tab)
    out = half_sums(1, BF16, y13o[0], y2o, y13o[1], wave_tab, part, keep)
    return out.reshape(steps, chans, chans, lags)


def solution(mesh):
    def body(traces, mask, plan):
        return per_device(8, traces, mask, plan)

    return jax.shard_map(
        body,
        mesh=mesh,
        in_specs=(P("blk", "seg", None), P("blk", None, None), P("blk", None)),
        out_specs=P("seg", "blk", None, None),
        check_vma=False,
    )
```

```python
import functools
import math

import jax
import jax.numpy as jnp
import ml_dtypes
import numpy as np
from jax import lax
from jax.experimental import pallas as pl
from jax.experimental.pallas import tpu as pltpu
from jax.sharding import PartitionSpec as P


EPS = 1e-05
TINY = 1e-30
STEPS = 4
F32 = jnp.float32
BF16 = jnp.bfloat16
VMEM = pl.BlockSpec(memory_space=pltpu.VMEM)
SMEM = pl.BlockSpec(memory_space=pltpu.SMEM)
HBM = pl.BlockSpec(memory_space=pltpu.HBM)
WIDTH = 256
REACH = 128
PARTS = 2


def angle_table(rows, cols, length):
    product = np.arange(rows)[:, None] * np.arange(cols)[None, :] % (2 * length)
    return product.astype(np.float32) * np.float32(math.pi / length)


def wave_table(length):
    angles = angle_table(length // 2, length, length)
    table = np.stack((np.cos(angles), np.sin(angles))).astype(ml_dtypes.bfloat16)
    return np.stack(np.split(table, PARTS, axis=2))


def fill_box(box_ref, half):
    left = lax.broadcasted_iota(jnp.int32, box_ref.shape, 0) - REACH
    right = lax.broadcasted_iota(jnp.int32, box_ref.shape, 1)
    box_ref[...] = jnp.where(jnp.abs(left - right) <= half, 1.0, 0.0).astype(BF16)


def box_sum(values, box, col):
    low = max(0, col - REACH)
    high = min(values.shape[1], col + WIDTH + REACH)
    tile = box[low - col + REACH : high - col + REACH, :]
    return jnp.dot(values[:, low:high], tile, preferred_element_type=F32)


def normalize_kernel(half, wins, traces_hbm, out_ref, traces_ref, mag_ref, box_ref, sems):
    rows, length = traces_ref.shape
    chans = rows // wins
    copies = []
    for q, col in enumerate(range(0, length, WIDTH)):
        cols = slice(col, col + WIDTH)
        copies.append(pltpu.make_async_copy(traces_hbm.at[:, cols], traces_ref.at[:, cols], sems.at[q]))
        copies[-1].start()
    fill_box(box_ref, half)
    target = lax.broadcasted_iota(jnp.int32, (rows, rows), 0)
    source = lax.broadcasted_iota(jnp.int32, (rows, rows), 1)
    order = jnp.where(target % chans * wins + target // chans == source, 1.0, 0.0).astype(BF16)
    for q in range(len(copies) + 1):
        if q < len(copies):
            copies[q].wait()
            cols = slice(q * WIDTH, (q + 1) * WIDTH)
            mag_ref[:, cols] = jnp.abs(traces_ref[:, cols]).astype(BF16)
        if q > 0:
            cols = slice((q - 1) * WIDTH, q * WIDTH)
            level = box_sum(mag_ref, box_ref, (q - 1) * WIDTH) / (2 * half + 1)
            normed = (traces_ref[:, cols] / (level + EPS)).astype(BF16)
            out_ref[:, cols] = jnp.dot(order, normed, preferred_element_type=F32).astype(BF16)


def start_tables(wave_hbm, wave_ref, sems):
    copies = [pltpu.make_async_copy(wave_hbm.at[q], wave_ref.at[q], sems.at[q]) for q in range(PARTS)]
    for copy in copies:
        copy.start()
    return copies


def whiten_into(x_refs, wave_ref, box_ref, amp_ref, work_ref, out_refs, half, copies):
    rows, length = x_refs[0].shape
    count = len(x_refs)
    mid = length // 2
    shape = out_refs[0].shape[1:3] + (WIDTH,)
    both = jnp.concatenate([ref[:, :mid] for ref in x_refs] + [ref[:, mid:] for ref in x_refs], axis=0)
    lane = lax.broadcasted_iota(jnp.int32, (1, WIDTH), 1)
    even = (lane & 1) == 0
    sign = (1 - (lane & 2)).astype(F32)
    top = count * rows
    for col in range(0, length, WIDTH):
        cols = slice(col, col + WIDTH)
        q, at = divmod(col, length // PARTS)
        if at == 0:
            copies[q].wait()
        cos_part = jnp.dot(both, wave_ref[q, 0, :, at : at + WIDTH], preferred_element_type=F32)
        sin_part = jnp.dot(both, wave_ref[q, 1, :, at : at + WIDTH], preferred_element_type=F32)
        re = cos_part[:top] + sign * jnp.where(even, cos_part[top:], -sin_part[top:])
        im = sin_part[:top] + sign * jnp.where(even, sin_part[top:], cos_part[top:])
        work_ref[0, :, cols] = re
        work_ref[1, :, cols] = im
        power = re * re + im * im
        amp_ref[:, cols] = (power * lax.rsqrt(jnp.maximum(power, TINY))).astype(BF16)
    for col in range(0, length, WIDTH):
        cols = slice(col, col + WIDTH)
        smooth = box_sum(amp_ref, box_ref, col) / (2 * half + 1)
        scale = 1.0 / (smooth + EPS)
        for c in range(2):
            white = work_ref[c, :, cols] * scale
            for n, ref in enumerate(out_refs):
                ref[c, :, :, cols] = white[n * rows : (n + 1) * rows].astype(ref.dtype).reshape(shape)


def whiten_kernel(half, x_ref, wave_hbm, out_ref, wave_ref, box_ref, amp_ref, work_ref, sems):
    copies = start_tables(wave_hbm, wave_ref, sems)
    fill_box(box_ref, half)
    whiten_into([x_ref], wave_ref, box_ref, amp_ref, work_ref, [out_ref], half, copies)


def cross_sums(mine_ref, far_ref, cross_ref, base):
    _, wins, chans, length = mine_ref.shape
    group = 8
    groups = chans // group

    def step(at, carry):
        lanes = pl.ds(pl.multiple_of(at // groups * 128, 128), 128)
        first = pl.multiple_of(at % groups * group, group)

        def add(w, sums):
            sums = list(sums)
            for c in range(2):
                far = far_ref[c, w, :, lanes]
                mine = mine_ref.at[c, w, pl.ds(first, group), lanes]
                for i in range(group):
                    sums[i] = sums[i] + mine[i : i + 1, :] * far
            return tuple(sums)

        zeros = tuple(jnp.zeros((chans, 128), F32) for _ in range(group))
        sums = lax.fori_loop(0, wins, add, zeros, unroll=8)
        total = jnp.concatenate(sums, axis=0).astype(BF16)
        cross_ref[pl.ds(base + pl.multiple_of(first * chans, group * chans), group * chans), lanes] = total
        return carry

    lax.fori_loop(0, length // 128 * groups, step, 0)


def flip_of(distance, per_row):
    blk = lax.axis_index("blk")
    chip = blk // 2
    core = blk % 2
    wrap = (chip % per_row == per_row - 1).astype(jnp.int32)
    ahead = ((chip + 1) % per_row == per_row - 1).astype(jnp.int32)
    one = jnp.where(core == 0, 0, wrap)
    three = jnp.where(core == 0, wrap, jnp.bitwise_xor(wrap, ahead))
    return jnp.where(distance == 1, one, jnp.where(distance == 2, wrap, jnp.where(distance == 3, three, 0)))


def half_kernel(
    half, per_row, second, scale, plan_ref, own_ref, other_ref, y1_ref, y2_ref, y3_ref, wave_hbm, *refs
):
    if second:
        part_ref, mask_ref, out_ref = refs[:3]
        refs = refs[3:]
    else:
        out_ref = refs[0]
        refs = refs[1:]
    wave_ref, box_ref, amp_ref, x_ref, work_ref, mine_ref, far_ref, cross_ref, sems = refs
    copies = start_tables(wave_hbm, wave_ref, sems)
    fill_box(box_ref, half)
    seg = lax.axis_index("seg")
    chans = own_ref.shape[2]
    wins = own_ref.shape[1]
    steps = out_ref.shape[0]
    pairs = chans * chans
    distances = [plan_ref[0, seg * steps + n] for n in range(steps)]

    for n, distance in enumerate(distances):
        which = jnp.bitwise_xor(flip_of(distance, per_row), second)
        for h, ref in enumerate((own_ref, other_ref)):

            @pl.when(which == h)
            def _(ref=ref, n=n):
                for c in range(2):
                    for w in range(wins):
                        mine_ref[n, c, w] = ref[c, w].astype(F32)

        for when, y_ref in ((distance == 1, y1_ref), (distance % 2 == 0, y2_ref), (distance == 3, y3_ref)):

            @pl.when(when)
            def _(y_ref=y_ref, n=n):
                x_ref[n] = y_ref[...]

    x_refs = [x_ref.at[n] for n in range(steps)]
    far_refs = [far_ref.at[n] for n in range(steps)]
    whiten_into(x_refs, wave_ref, box_ref, amp_ref, work_ref, far_refs, half, copies)

    for n, distance in enumerate(distances):

        @pl.when(distance == 0)
        def _(n=n):
            far_ref[n] = mine_ref[n]

        cross_sums(mine_ref.at[n], far_ref.at[n], cross_ref, n * pairs)

    lane = lax.broadcasted_iota(jnp.int32, (1, 128), 1)
    cross_ref[:, :128] = cross_ref[:, :128] * jnp.where(lane == 0, 0.5, 1.0).astype(BF16)
    folded = lax.dot_general(
        cross_ref[...], jnp.concatenate([wave_ref[q, 0] for q in range(PARTS)], axis=1), (((1,), (1,)), ((), ())), preferred_element_type=F32
    )
    for n, distance in enumerate(distances):
        rows = slice(n * pairs, (n + 1) * pairs)
        if second:
            keep = mask_ref[distance]
            for col in range(0, folded.shape[1], 128):
                cols = slice(col, col + 128)
                part = folded[rows, cols] * (2.0 * scale) + part_ref[n, :, cols]
                part = part * keep
                out_ref[n, :, cols] = part.astype(BF16)
        else:
            out_ref[n] = folded[rows] * (2.0 * scale)


def per_device(per_row, traces, mask, plan):
    chans, wins, length = traces.shape
    half = length // 16
    lags = length // 2
    rows = chans * wins
    blocks = lax.axis_size("blk")
    segs = lax.axis_size("seg")
    steps = STEPS // segs

    def send(array, source):
        pairs = []
        for b in range(blocks):
            for s in range(segs):
                where = source(b, s)
                if where is not None and where[0] < blocks:
                    pairs.append((where[0] * segs + where[1], b * segs + s))
        return lax.ppermute(array, ("blk", "seg"), pairs)

    def ahead(b, s, by):
        chip = b // 2
        wraps = (chip % per_row == per_row - 1) and (b + by) // 2 > chip
        return (b + by, 1 - s if wraps else s)

    def in_hbm(array):
        return pltpu.with_memory_space_constraint(array, pltpu.HBM)

    wave_tab = in_hbm(jnp.asarray(wave_table(length)))
    white_shape = (2, wins, chans, length)
    scale = 1.0 / math.sqrt(wins * segs * length)
    quarters = length // WIDTH
    box = pltpu.VMEM((WIDTH + 2 * REACH, WIDTH), BF16)
    wave = pltpu.VMEM(wave_tab.shape, BF16)
    amp = pltpu.VMEM((rows, length), BF16)
    work = pltpu.VMEM((2, rows, length), F32)

    x = pl.pallas_call(
        functools.partial(normalize_kernel, half, wins),
        out_shape=jax.ShapeDtypeStruct((rows, length), BF16),
        in_specs=[HBM],
        out_specs=VMEM,
        scratch_shapes=[
            pltpu.VMEM((rows, length), F32),
            amp,
            box,
            pltpu.SemaphoreType.DMA((quarters,)),
        ],
        compiler_params=pltpu.CompilerParams(vmem_limit_bytes=6 << 20),
        name="normalize",
    )(in_hbm(traces.reshape(rows, length)))

    def whiten(array):
        return pl.pallas_call(
            functools.partial(whiten_kernel, half),
            out_shape=jax.ShapeDtypeStruct(white_shape, BF16),
            in_specs=[VMEM, HBM],
            out_specs=VMEM,
            scratch_shapes=[wave, box, amp, work, pltpu.SemaphoreType.DMA((quarters,))],
            compiler_params=pltpu.CompilerParams(vmem_limit_bytes=12 << 20),
            name="whiten",
        )(array, wave_tab)

    def half_sums(second, dtype, *args):
        return pl.pallas_call(
            functools.partial(half_kernel, half, per_row, second, scale),
            out_shape=jax.ShapeDtypeStruct((steps, chans * chans, lags), dtype),
            in_specs=[SMEM] + [VMEM] * 5 + [HBM] + [VMEM] * (2 * second),
            out_specs=VMEM,
            scratch_shapes=[
                wave,
                box,
                pltpu.VMEM((steps * rows, length), BF16),
                pltpu.VMEM((steps, rows, length), BF16),
                pltpu.VMEM((2, steps * rows, length), F32),
                pltpu.VMEM((steps,) + white_shape, F32),
                pltpu.VMEM((steps,) + white_shape, F32),
                pltpu.VMEM((steps * chans * chans, length), BF16),
                pltpu.SemaphoreType.DMA((quarters,)),
            ],
            compiler_params=pltpu.CompilerParams(vmem_limit_bytes=24 << 20),
            name="second" if second else "first",
        )(plan, own, other, *args)

    keep = jnp.transpose(mask, (1, 0, 2)).reshape(STEPS, chans * chans, 1)
    keep = jnp.broadcast_to(keep, (STEPS, chans * chans, 128)).astype(F32)

    def next_block(b, s):
        return ahead(b, s, 1) if b % 2 else (b + 1, s)

    y2 = send(x, lambda b, s: ahead(b, s, 2))
    o = send(x, lambda b, s: (b, 1 - s))
    y1 = send(x, next_block)
    own = whiten(x)
    y2, own = lax.optimization_barrier((y2, own))
    y2o = send(y2, lambda b, s: (b, 1 - s))
    y3 = send(y2, next_block)
    other = whiten(o)
    y2o, other = lax.optimization_barrier((y2o, other))
    y13o = send(jnp.stack((o, y2o)), next_block)
    part = half_sums(0, F32, y1, y2, y3, wave_tab)
    out = half_sums(1, BF16, y13o[0], y2o, y13o[1], wave_tab, part, keep)
    return out.reshape(steps, chans, chans, lags)


def solution(mesh):
    def body(traces, mask, plan):
        return per_device(8, traces, mask, plan)

    return jax.shard_map(
        body,
        mesh=mesh,
        in_specs=(P("blk", "seg", None), P("blk", None, None), P("blk", None)),
        out_specs=P("seg", "blk", None, None),
        check_vma=False,
    )
```
